128 devices in a mesh: joined: 8 (over z, core), view: 16 (over y, x).
Axes of the slice: x: 4, y: 4, z: 4, core: 2. Of those that a mesh axis runs over, the one named last changes fastest.
Arguments:
- estimate: float32 [16, 1024, 2048], P('view', 'joined'), may hold values from 0.5 to 2
- views: float32 [16, 8, 1024, 2048], P('view', None, 'joined'), may hold values from 0.25 to 4
- psf: float32 [8, 2, 65], replicated, may hold values from 0.2 to 2
- offsets: int32 [8, 2], replicated, may hold values from -16 to 16, as said below
- lengths: int32 [8, 2], replicated, may hold values from 1 to 8, as said below
Outputs:
- deconvolved: float32 [16, 1024, 2048], P('view', 'joined')
The draws below stay inside these ranges and needn't reach their ends.
Inputs may be any that keep to these rules, and one draw needn't show every extreme that they name: `offsets`: offsets along each lateral dimension reach both -16 and 16 in every draw. `lengths`: in every depth block some view has all 8 planes.
All inputs are finite; a program needn't handle non-finite values.
Results may differ from the reference program's by a relative error of at most 0.0001.
Values sent between devices are 32-bit elements; how exact they have to be, the bound alone decides.
A program may use at most 128 MiB of HBM per device.

```python
import math
import jax
import jax.numpy as jnp

TAPS = 65
MAXD = 16
RADIUS = 32
BLOCKS = 2
ITERS = 1
NY = 2048
VIEWS = 8
ZB = 8
DEPTH = 16
NX = 1024


def draw_offsets(key, part):
    first, second, third = jax.random.split(jax.random.fold_in(key, 11), 3)
    values = jax.random.randint(first, (VIEWS, 2), -MAXD, MAXD + 1)
    upper = jax.random.randint(second, (2,), 0, VIEWS)
    step_on = jax.random.randint(third, (2,), 1, max(VIEWS, 2))
    lower = jnp.mod(upper + step_on, VIEWS)
    members = jnp.arange(VIEWS, dtype=jnp.int32)[:, None]
    values = jnp.where(members == lower[None, :], -MAXD, values)
    values = jnp.where(members == upper[None, :], MAXD, values)
    return values.astype(jnp.int32)


def draw_lengths(key, part):
    first, second = jax.random.split(jax.random.fold_in(key, 23), 2)
    values = jax.random.randint(first, (VIEWS, BLOCKS), 1, ZB + 1)
    full_member = jax.random.randint(second, (BLOCKS,), 0, VIEWS)
    members = jnp.arange(VIEWS, dtype=jnp.int32)[:, None]
    values = jnp.where(members == full_member[None, :], ZB, values)
    return values.astype(jnp.int32)


def shard_levels(key, shape, pieces, least, top_value):
    gain = 1.0
    for dim, blocks in pieces:
        heights = jax.random.uniform(jax.random.fold_in(jax.random.fold_in(key, 6), dim), (blocks,), jnp.float32, least / len(pieces), top_value / len(pieces))
        gain = gain * jnp.repeat(jnp.exp(heights), shape[dim] // blocks).reshape((-1,) + (1,) * (len(shape) - 1 - dim))
    return gain


def setup_inputs(seed: int = 0) -> dict:
    key_of = jax.random.split(jax.random.key(seed), 6)
    return {
        "estimate": jnp.clip(jnp.exp(math.log(2.0) - 1.3862944 * jax.random.uniform(key_of[0], (DEPTH, NX, NY), jnp.float32) ** shard_levels(key_of[0], (DEPTH, NX, NY), ((0, 16), (1, 8)), -0.2, 0.2)), 0.5, 2.0),
        "views": jnp.clip(jnp.exp(math.log(4.0) - 2.7725887 * jax.random.uniform(key_of[1], (VIEWS * BLOCKS, ZB, NX, NY), jnp.float32) ** shard_levels(key_of[1], (VIEWS * BLOCKS, ZB, NX, NY), ((0, 16), (2, 8)), -0.2, 0.2)), 0.25, 4.0),
        "psf": jnp.clip(jnp.exp(jax.random.uniform(key_of[2], (VIEWS, 2, TAPS), jnp.float32, math.log(0.2), math.log(2.0))), 0.2, 2.0),
        "offsets": draw_offsets(jax.random.fold_in(key_of[5], 71), 0),
        "lengths": draw_lengths(jax.random.fold_in(key_of[5], 71), 0),
    }


def line_kernel(taps, shift, length):
    index = jnp.mod(RADIUS - jnp.arange(TAPS, dtype=jnp.int32) - shift, length)
    return jnp.zeros((length,), jnp.float32).at[index].add(taps)


def reference(estimate, views, psf, offsets, lengths):
    stacks = views.reshape(VIEWS, BLOCKS, ZB, NX, NY)
    planes = jnp.arange(ZB, dtype=jnp.int32)
    live = (planes[None, None, :] < lengths[:, :, None]).astype(jnp.float32)
    count = jnp.sum(live, axis=0)
    spectra = []
    for member in range(VIEWS):
        kernel_x = psf[member, 0] / jnp.sum(psf[member, 0])
        kernel_y = psf[member, 1] / jnp.sum(psf[member, 1])
        line_x = line_kernel(kernel_x, offsets[member, 0], NX)
        line_y = line_kernel(kernel_y, offsets[member, 1], NY)
        spectra.append(jnp.fft.rfft2(line_x[:, None] * line_y[None, :]))
    current = estimate.reshape(BLOCKS, ZB, NX, NY)
    for step in range(ITERS):
        transform = jnp.fft.rfft2(current, axes=(-2, -1))
        correction = jnp.zeros_like(current)
        for member in range(VIEWS):
            image = jnp.fft.irfft2(transform * spectra[member], s=(NX, NY), axes=(-2, -1))
            ratio = live[member][:, :, None, None] * stacks[member] / image
            back = jnp.fft.irfft2(jnp.fft.rfft2(ratio, axes=(-2, -1)) * jnp.conj(spectra[member]), s=(NX, NY), axes=(-2, -1))
            correction = correction + back
        current = current * correction / count[:, :, None, None]
    return current.reshape(DEPTH, NX, NY)
```

```python
import jax
import jax.numpy as jnp
from jax import lax
from jax.experimental import pallas as pl
from jax.experimental.pallas import tpu as pltpu
from jax.sharding import PartitionSpec as P

MESH = pl.DeviceIdType.MESH
VIEWS = 8
BLOCKS = 2
ZB = 8
TAPS = 65
REACH = 48
TILE = 128
COLS = 2048
SPAN = TILE + 2 * REACH
PADDED = COLS + 128
UNIT = 16
ORDER = (0, 1, 2, 5, 6, 7, 3, 4)
CHUNKS = len(ORDER)
GROUPS = CHUNKS // 2
STEPS = (1, 3, 2)


def split(value):
    high = value.astype(jnp.bfloat16)
    low = (value - high.astype(jnp.float32)).astype(jnp.bfloat16)
    return high, low


def dot(a, b):
    return jnp.dot(a, b, preferred_element_type=jnp.float32)


def kernel(
    est_ref, views_ref, taps_ref, out_ref,
    arr, image, est, est_hi, est_lo, win_hi, win_lo, bwin_hi, bwin_lo,
    spread_hi, spread_lo, acc, edges, band_x, band_xt, band_f, band_b, rows_x,
    x_sem, y_sem, r_sem, e_sem, es_sem, c_sem, cs_sem, l_sem,
):
    tile = lax.axis_index("joined")
    position = lax.axis_index("view")
    y = position // 4
    x = position % 4
    tiles = 8
    up = lax.rem(tile + 1, tiles)
    down = lax.rem(tile + tiles - 1, tiles)

    barrier = pltpu.get_barrier_semaphore()
    peers = [(tile, y * 4 + (x + d) % 4) for d in (1, 2, 3)]
    peers += [(tile, ((y + d) % 4) * 4 + x) for d in (1, 2, 3)]
    peers += [(up, position), (down, position)]
    for peer in peers:
        pl.semaphore_signal(barrier, inc=1, device_id=peer, device_id_type=MESH)
    pl.semaphore_wait(barrier, len(peers))

    def halo(side):
        if side == 0:
            return pltpu.make_async_remote_copy(
                est_ref.at[0, pl.ds(TILE - REACH, REACH)], est.at[pl.ds(0, REACH)],
                es_sem.at[0], e_sem.at[0], device_id=(up, position), device_id_type=MESH)
        return pltpu.make_async_remote_copy(
            est_ref.at[0, pl.ds(0, REACH)], est.at[pl.ds(REACH + TILE, REACH)],
            es_sem.at[1], e_sem.at[1], device_id=(down, position), device_id_type=MESH)

    halo(0).start()
    halo(1).start()
    own_est = pltpu.make_async_copy(est_ref.at[0], est.at[pl.ds(REACH, TILE)], l_sem)
    own_est.start()

    def side_of(turn):
        return (turn + y + 1) % 2

    def x_copy(index, turn, c):
        rows = pl.ds(ORDER[c] * UNIT, UNIT)
        h = side_of(turn)
        x2 = (x + STEPS[index]) % 4
        y2 = BLOCKS * (x % 2) + h
        slot = jnp.where(y2 == y, 2 * y + x // 2, VIEWS + 2 * x + h)
        return pltpu.make_async_remote_copy(
            views_ref.at[0, 4 * h + x2, rows], arr.at[slot, rows],
            x_sem.at[index, turn, c], r_sem.at[slot, c],
            device_id=(tile, y * 4 + x2), device_id_type=MESH)

    def y_copy(step, turn, c):
        rows = pl.ds(ORDER[c] * UNIT, UNIT)
        h = side_of(turn)
        xs = (x - step) % 4
        y2 = BLOCKS * (xs % 2) + h
        k = 2 * y + xs // 2
        slot = VIEWS + 2 * xs + h
        source = views_ref.at[0, 4 * h + x, rows] if step == 0 else arr.at[slot, rows]
        remote = pltpu.make_async_remote_copy(
            source, arr.at[k, rows], y_sem.at[step, turn, c], r_sem.at[k, c],
            device_id=(tile, y2 * 4 + x), device_id_type=MESH)
        local = pltpu.make_async_copy(source, arr.at[k, rows], r_sem.at[k, c])
        return y2 != y, slot, remote, local

    def arrived(slot, c):
        rows = pl.ds(ORDER[c] * UNIT, UNIT)
        pltpu.make_async_copy(
            views_ref.at[0, 0, rows], arr.at[slot, rows], r_sem.at[slot, c]).wait()

    for c in range(CHUNKS):
        for index in range(3):
            for turn in range(2):
                x_copy(index, turn, c).start()
    for c in range(CHUNKS):
        for turn in range(2):
            away, _, remote, local = y_copy(0, turn, c)

            @pl.when(away)
            def _():
                remote.start()

            @pl.when(jnp.logical_not(away))
            def _():
                local.start()

    def relay(c):
        for turn in range(2):
            for step in STEPS:
                away, slot, remote, _ = y_copy(step, turn, c)

                @pl.when(away)
                def _():
                    arrived(slot, c)
                    remote.start()

    @pl.loop(0, VIEWS)
    def _(k):
        row = jnp.broadcast_to(taps_ref[pl.ds(k, 1), :], (TILE, 256))
        band = pltpu.roll(row, 0, 1, stride=1, stride_axis=0)
        rows_x[k] = band
        high, low = split(band)
        band_x[k, 0:TILE, :] = high
        band_x[k, TILE : 2 * TILE, :] = low
        for first, target in ((VIEWS, band_f), (2 * VIEWS, band_b)):
            row = jnp.broadcast_to(taps_ref[pl.ds(first + k, 1), :], (256, 256))
            band = pltpu.roll(row, 0, 1, stride=1, stride_axis=0)[:, :128]
            high, low = split(band)
            target[k, :, 0:128] = high
            target[k, :, 128:256] = low

    for g in range(GROUPS):
        first, second = ORDER[2 * g] * UNIT, ORDER[2 * g + 1] * UNIT
        picked = jnp.concatenate(
            [rows_x[:, first : first + UNIT, :], rows_x[:, second : second + UNIT, :]], axis=1)
        band = jnp.transpose(picked.reshape(256, 256))
        high, low = split(band)
        band_xt[g, 0:256, :] = high
        band_xt[g, 256:512, :] = low

    own_est.wait()
    halo(0).wait_recv()
    halo(1).wait_recv()
    est[SPAN:256, :] = jnp.zeros((256 - SPAN, COLS), jnp.float32)

    @pl.loop(0, 256 // 32)
    def _(i):
        rows = pl.ds(pl.multiple_of(i * 32, 32), 32)
        high, low = split(pltpu.roll(est[rows, :], 64, 1))
        est_hi[rows, 0:COLS] = high
        est_lo[rows, 0:COLS] = low
        est_hi[rows, COLS:PADDED] = high[:, 0:128]
        est_lo[rows, COLS:PADDED] = low[:, 0:128]

    @pl.loop(0, VIEWS)
    def _(k):
        for first in range(0, PADDED, 256):
            width = min(256, PADDED - first)
            cols = pl.ds(first, width)
            wide = dot(band_x[k], est_hi[:, cols])
            value = wide[:TILE] + wide[TILE:] + dot(band_x[k, 0:TILE, :], est_lo[:, cols])
            high, low = split(value)
            for part in range(width // 128):
                b = first // 128 + part
                piece = slice(128 * part, 128 * part + 128)
                if b < 16:
                    win_hi[b, :, 0:128] = high[:, piece]
                    win_lo[b, :, 0:128] = low[:, piece]
                if b > 0:
                    win_hi[b - 1, :, 128:256] = high[:, piece]
                    win_lo[b - 1, :, 128:256] = low[:, piece]
        for b in range(0, 16, 4):
            wide = dot(win_hi[b : b + 4].reshape(512, 256), band_f[k])
            value = wide[:, :128] + wide[:, 128:]
            value = value + dot(win_lo[b : b + 4].reshape(512, 256), band_f[k, :, 0:128])
            for part in range(4):
                image[k, :, 128 * (b + part) : 128 * (b + part) + 128] = value[
                    128 * part : 128 * part + 128]

    def backward(g):
        first, second = ORDER[2 * g] * UNIT, ORDER[2 * g + 1] * UNIT

        @pl.loop(0, VIEWS)
        def _(k):
            arrived(k, 2 * g)
            arrived(k, 2 * g + 1)
            for half, start in ((0, first), (1, second)):
                rows = slice(start, start + UNIT)
                ratio = arr[k, rows, :] / image[k, rows, :]
                high, low = split(pltpu.roll(ratio, 64, 1))
                into = slice(half * UNIT, half * UNIT + UNIT)
                for b in range(16):
                    piece = slice(128 * b, 128 * b + 128)
                    before = (b - 1) % 16
                    bwin_hi[b, into, 0:128] = high[:, piece]
                    bwin_lo[b, into, 0:128] = low[:, piece]
                    bwin_hi[before, into, 128:256] = high[:, piece]
                    bwin_lo[before, into, 128:256] = low[:, piece]
            wide = dot(bwin_hi[...].reshape(512, 256), band_b[k])
            value = wide[:, :128] + wide[:, 128:]
            value = value + dot(bwin_lo[...].reshape(512, 256), band_b[k, :, 0:128])
            high, low = split(value)
            for b in range(16):
                spread_hi[k, :, 128 * b : 128 * b + 128] = high[32 * b : 32 * b + 32]
                spread_lo[k, :, 128 * b : 128 * b + 128] = low[32 * b : 32 * b + 32]

        inner = g == GROUPS - 1
        base, count = (REACH, TILE) if inner else (0, 256)
        for start in range(0, COLS, 256):
            cols = slice(start, start + 256)
            high = spread_hi[:, :, cols].reshape(256, 256)
            low = spread_lo[:, :, cols].reshape(256, 256)
            value = dot(band_xt[g, base : base + count, :], high)
            value = value + dot(band_xt[g, 256 + base : 256 + base + count, :], high)
            value = value + dot(band_xt[g, base : base + count, :], low)
            if g == 0:
                acc[:, cols] = value
            else:
                acc[base : base + count, cols] += value

    def edge(side):
        if side == 0:
            return pltpu.make_async_remote_copy(
                acc.at[pl.ds(REACH + TILE, REACH)], edges.at[0],
                cs_sem.at[0], c_sem.at[0], device_id=(up, position), device_id_type=MESH)
        return pltpu.make_async_remote_copy(
            acc.at[pl.ds(0, REACH)], edges.at[1],
            cs_sem.at[1], c_sem.at[1], device_id=(down, position), device_id_type=MESH)

    relay(0)
    relay(1)
    relay(2)
    backward(0)
    relay(3)
    relay(4)
    backward(1)
    relay(5)
    relay(6)
    backward(2)
    relay(7)
    edge(0).start()
    edge(1).start()
    backward(3)
    edge(0).wait_recv()
    edge(1).wait_recv()
    count = jnp.broadcast_to(taps_ref[3 * VIEWS : 3 * VIEWS + 1, 0:128], (UNIT, 128))
    for part in range(TILE // UNIT):
        rows = slice(REACH + part * UNIT, REACH + part * UNIT + UNIT)
        total = acc[rows, :]
        if part < REACH // UNIT:
            total = total + edges[0, part * UNIT : part * UNIT + UNIT, :]
        if part >= (TILE - REACH) // UNIT:
            low_row = part * UNIT - (TILE - REACH)
            total = total + edges[1, low_row : low_row + UNIT, :]
        value = est[rows, :] * total
        for b in range(16):
            cols = slice(128 * b, 128 * b + 128)
            out_ref[0, part * UNIT : part * UNIT + UNIT, cols] = value[:, cols] / count

    halo(0).wait_send()
    halo(1).wait_send()
    edge(0).wait_send()
    edge(1).wait_send()
    for c in range(CHUNKS):
        for turn in range(2):
            for index in range(3):
                x_copy(index, turn, c).wait_send()
            for step in range(4):
                away, _, remote, _ = y_copy(step, turn, c)

                @pl.when(away)
                def _():
                    remote.wait_send()


def prepare(psf, offsets, lengths):
    position = lax.axis_index("view")
    block, row = position // ZB, position % ZB
    kernels = psf / jnp.sum(psf, axis=2, keepdims=True)
    block_lengths = lax.dynamic_index_in_dim(lengths, block, 1, keepdims=False)
    live = (row < block_lengths).astype(jnp.float32)
    lane = jnp.arange(256, dtype=jnp.int32)[None, :]
    tap = jnp.arange(TAPS, dtype=jnp.int32)
    dx, dy = offsets[:, 0:1], offsets[:, 1:2]

    def place(index, taps):
        onehot = index[:, :, None] == tap[None, None, :]
        return jnp.sum(jnp.where(onehot, taps[:, None, :], 0.0), axis=2)

    rows = [
        place(lane - 16 - dx, kernels[:, 0]),
        place(224 - lane - dy, kernels[:, 1]),
        place(lane - 160 - dy, kernels[:, 1] * live[:, None]),
        jnp.full((VIEWS, 256), jnp.sum(live), jnp.float32),
    ]
    return jnp.concatenate(rows, axis=0)


def per_device(estimate, views, psf, offsets, lengths):
    taps = prepare(psf, offsets, lengths)
    f32, bf16 = jnp.float32, jnp.bfloat16
    anywhere = pl.BlockSpec(memory_space=pl.ANY)
    vmem = pl.BlockSpec(memory_space=pltpu.VMEM)
    dma = pltpu.SemaphoreType.DMA
    return pl.pallas_call(
        kernel,
        out_shape=jax.ShapeDtypeStruct(estimate.shape, f32),
        in_specs=[anywhere, anywhere, vmem],
        out_specs=vmem,
        scratch_shapes=[
            pltpu.VMEM((2 * VIEWS, TILE, COLS), f32),
            pltpu.VMEM((VIEWS, TILE, COLS), f32),
            pltpu.VMEM((256, COLS), f32),
            pltpu.VMEM((256, PADDED), bf16),
            pltpu.VMEM((256, PADDED), bf16),
            pltpu.VMEM((16, TILE, 256), bf16),
            pltpu.VMEM((16, TILE, 256), bf16),
            pltpu.VMEM((16, 2 * UNIT, 256), bf16),
            pltpu.VMEM((16, 2 * UNIT, 256), bf16),
            pltpu.VMEM((VIEWS, 2 * UNIT, COLS), bf16),
            pltpu.VMEM((VIEWS, 2 * UNIT, COLS), bf16),
            pltpu.VMEM((256, COLS), f32),
            pltpu.VMEM((2, REACH, COLS), f32),
            pltpu.VMEM((VIEWS, 2 * TILE, 256), bf16),
            pltpu.VMEM((GROUPS, 512, 256), bf16),
            pltpu.VMEM((VIEWS, 256, 256), bf16),
            pltpu.VMEM((VIEWS, 256, 256), bf16),
            pltpu.VMEM((VIEWS, TILE, 256), f32),
            dma((3, 2, CHUNKS)),
            dma((4, 2, CHUNKS)),
            dma((2 * VIEWS, CHUNKS)),
            dma((2,)),
            dma((2,)),
            dma((2,)),
            dma((2,)),
            dma,
        ],
        compiler_params=pltpu.CompilerParams(
            collective_id=0, has_side_effects=True, vmem_limit_bytes=60 * 2**20
        ),
        name="deconvolve",
    )(estimate, views, taps)


def solution(mesh):
    return jax.shard_map(
        per_device,
        mesh=mesh,
        in_specs=(P("view", "joined", None), P("view", None, "joined", None), P(), P(), P()),
        out_specs=P("view", "joined", None),
        check_vma=False,
    )
```

```python
import jax
import jax.numpy as jnp
from jax import lax
from jax.experimental import pallas as pl
from jax.experimental.pallas import tpu as pltpu
from jax.sharding import PartitionSpec as P

MESH = pl.DeviceIdType.MESH
VIEWS = 8
BLOCKS = 2
ZB = 8
TAPS = 65
REACH = 48
TILE = 128
COLS = 2048
SPAN = TILE + 2 * REACH
PADDED = COLS + 128
UNIT = 16
ORDER = (0, 1, 2, 5, 6, 7, 3, 4)
CHUNKS = len(ORDER)
GROUPS = CHUNKS // 2
STEPS = (1, 3, 2)
AHEAD = 3
LAG = 1
SKEW = 1


def travel():
    turns = []
    for t in range(CHUNKS + SKEW):
        if t < CHUNKS:
            turns.append((t, (1, 3)))
        if t >= SKEW:
            turns.append((t - SKEW, (2,)))
    return turns


def plan():
    items, done = [], 0
    for index, (c, steps) in enumerate(TRAVEL):
        if index == 0:
            items.append(("forward", 0, 4))
        items.append(("relay", c, steps))
        if 1 in steps and c + AHEAD < CHUNKS:
            items.append(("own", c + AHEAD))
        if index == 1:
            items.append(("forward", 4, VIEWS))
        if 2 in steps:
            ready = c - LAG if c < CHUNKS - 1 else CHUNKS - 1
            while done <= ready:
                if done == CHUNKS - 2:
                    items.append(("edge",))
                items.append(("y", done))
                if done % 2:
                    items.append(("x", done // 2))
                done += 1
    return items


TRAVEL = travel()
PLAN = plan()


def split(value):
    high = value.astype(jnp.bfloat16)
    low = (value - high.astype(jnp.float32)).astype(jnp.bfloat16)
    return high, low


def dot(a, b):
    return jnp.dot(a, b, preferred_element_type=jnp.float32)


def kernel(
    est_ref, views_ref, psf_ref, offsets_ref, lengths_ref, out_ref,
    arr, image, est, est_hi, est_lo, win_hi, win_lo, bwin_hi, bwin_lo,
    spread_hi, spread_lo, acc, edges, band_x, band_xt, band_f, band_b, rows_x, taps_ref,
    x_sem, y_sem, r_sem, e_sem, es_sem, c_sem, cs_sem, l_sem,
):
    tile = lax.axis_index("joined")
    position = lax.axis_index("view")
    y = position // 4
    x = position % 4
    tiles = 8
    up = lax.rem(tile + 1, tiles)
    down = lax.rem(tile + tiles - 1, tiles)

    barrier = pltpu.get_barrier_semaphore()
    peers = [(tile, y * 4 + (x + d) % 4) for d in (1, 2, 3)]
    peers += [(tile, ((y + d) % 4) * 4 + x) for d in (1, 2, 3)]
    peers += [(up, position), (down, position)]
    for peer in peers:
        pl.semaphore_signal(barrier, inc=1, device_id=peer, device_id_type=MESH)
    pl.semaphore_wait(barrier, len(peers))

    def halo(side):
        if side == 0:
            return pltpu.make_async_remote_copy(
                est_ref.at[0, pl.ds(TILE - REACH, REACH)], est.at[pl.ds(0, REACH)],
                es_sem.at[0], e_sem.at[0], device_id=(up, position), device_id_type=MESH)
        return pltpu.make_async_remote_copy(
            est_ref.at[0, pl.ds(0, REACH)], est.at[pl.ds(REACH + TILE, REACH)],
            es_sem.at[1], e_sem.at[1], device_id=(down, position), device_id_type=MESH)

    halo(0).start()
    halo(1).start()
    own_est = pltpu.make_async_copy(est_ref.at[0], est.at[pl.ds(REACH, TILE)], l_sem)
    own_est.start()

    def side_of(turn):
        return (turn + y + 1) % 2

    def x_copy(index, turn, c):
        rows = pl.ds(ORDER[c] * UNIT, UNIT)
        h = side_of(turn)
        x2 = (x + STEPS[index]) % 4
        y2 = BLOCKS * (x % 2) + h
        slot = jnp.where(y2 == y, 2 * y + x // 2, VIEWS + 2 * x + h)
        return pltpu.make_async_remote_copy(
            views_ref.at[0, 4 * h + x2, rows], arr.at[slot, rows],
            x_sem.at[index, turn, c], r_sem.at[slot, c],
            device_id=(tile, y * 4 + x2), device_id_type=MESH)

    def y_route(step, turn, c):
        h = side_of(turn)
        xs = (x - step) % 4
        y2 = BLOCKS * (xs % 2) + h
        return pl.ds(ORDER[c] * UNIT, UNIT), h, xs, y2, 2 * y + xs // 2

    def y_copy(step, turn, c):
        rows, h, xs, y2, k = y_route(step, turn, c)
        source = views_ref.at[0, 4 * h + x, rows] if step == 0 else arr.at[VIEWS + 2 * xs + h, rows]
        return pltpu.make_async_remote_copy(
            source, arr.at[k, rows], y_sem.at[step, turn, c], r_sem.at[k, c],
            device_id=(tile, y2 * 4 + x), device_id_type=MESH)

    def arrived(slot, c):
        rows = pl.ds(ORDER[c] * UNIT, UNIT)
        pltpu.make_async_copy(
            views_ref.at[0, 0, rows], arr.at[slot, rows], r_sem.at[slot, c]).wait()

    def own(c):
        for turn in range(2):
            rows, h, _, y2, k = y_route(0, turn, c)

            @pl.when(y2 != y)
            def _():
                y_copy(0, turn, c).start()

            @pl.when(y2 == y)
            def _():
                pltpu.make_async_copy(
                    views_ref.at[0, 4 * h + x, rows], arr.at[k, rows], r_sem.at[k, c]).start()

    def relay(c, steps):
        for turn in range(2):
            for step in steps:
                _, h, xs, y2, _ = y_route(step, turn, c)

                @pl.when(y2 != y)
                def _():
                    arrived(VIEWS + 2 * xs + h, c)
                    y_copy(step, turn, c).start()

    for c, steps in TRAVEL:
        for index, step in enumerate(STEPS):
            if step in steps:
                for turn in range(2):
                    x_copy(index, turn, c).start()
    for c in range(AHEAD):
        own(c)

    block, plane_row = position // ZB, position % ZB
    blank = jnp.zeros((VIEWS, 128 - TAPS), jnp.float32)
    columns = []
    for axis in range(2):
        taps = psf_ref[:, axis, :]
        taps = taps / jnp.sum(taps, axis=1, keepdims=True)
        columns.append(jnp.transpose(jnp.concatenate([taps, blank], axis=1)))
    tap = lax.broadcasted_iota(jnp.int32, (128, 256), 0)
    lane = lax.broadcasted_iota(jnp.int32, (128, 256), 1)
    total = jnp.zeros((VIEWS, 256), jnp.float32)
    for k in range(VIEWS):
        live = jnp.where(plane_row < lengths_ref[k, block], 1.0, 0.0)
        total = total + live
        dx, dy = offsets_ref[k, 0], offsets_ref[k, 1]
        places = ((0, lane - 16 - dx), (1, 224 - lane - dy), (1, lane - 160 - dy))
        for kind, (axis, place) in enumerate(places):
            column = jnp.broadcast_to(columns[axis][:, k : k + 1], (128, 256))
            line = jnp.sum(jnp.where(place == tap, column, 0.0), axis=0, keepdims=True)
            if kind == 2:
                line = line * live
            taps_ref[kind * VIEWS + k : kind * VIEWS + k + 1, :] = line
    taps_ref[3 * VIEWS : 4 * VIEWS, :] = total

    @pl.loop(0, VIEWS)
    def _(k):
        row = jnp.broadcast_to(taps_ref[pl.ds(k, 1), :], (TILE, 256))
        band = pltpu.roll(row, 0, 1, stride=1, stride_axis=0)
        rows_x[k] = band
        high, low = split(band)
        band_x[k, 0:TILE, :] = high
        band_x[k, TILE : 2 * TILE, :] = low
        for first, target in ((VIEWS, band_f), (2 * VIEWS, band_b)):
            row = jnp.broadcast_to(taps_ref[pl.ds(first + k, 1), :], (256, 256))
            band = pltpu.roll(row, 0, 1, stride=1, stride_axis=0)[:, :128]
            high, low = split(band)
            target[k, :, 0:128] = high
            target[k, :, 128:256] = low

    for g in range(GROUPS):
        first, second = ORDER[2 * g] * UNIT, ORDER[2 * g + 1] * UNIT
        picked = jnp.concatenate(
            [rows_x[:, first : first + UNIT, :], rows_x[:, second : second + UNIT, :]], axis=1)
        band = jnp.transpose(picked.reshape(256, 256))
        high, low = split(band)
        band_xt[g, 0:256, :] = high
        band_xt[g, 256:512, :] = low

    own_est.wait()
    halo(0).wait_recv()
    halo(1).wait_recv()
    est[SPAN:256, :] = jnp.zeros((256 - SPAN, COLS), jnp.float32)

    @pl.loop(0, 256 // 32)
    def _(i):
        rows = pl.ds(pl.multiple_of(i * 32, 32), 32)
        high, low = split(pltpu.roll(est[rows, :], 64, 1))
        est_hi[rows, 0:COLS] = high
        est_lo[rows, 0:COLS] = low
        est_hi[rows, COLS:PADDED] = high[:, 0:128]
        est_lo[rows, COLS:PADDED] = low[:, 0:128]

    def forward(k):
        for first in range(0, PADDED, 256):
            width = min(256, PADDED - first)
            cols = pl.ds(first, width)
            wide = dot(band_x[k], est_hi[:, cols])
            value = wide[:TILE] + wide[TILE:] + dot(band_x[k, 0:TILE, :], est_lo[:, cols])
            high, low = split(value)
            for part in range(width // 128):
                b = first // 128 + part
                piece = slice(128 * part, 128 * part + 128)
                if b < 16:
                    win_hi[b, :, 0:128] = high[:, piece]
                    win_lo[b, :, 0:128] = low[:, piece]
                if b > 0:
                    win_hi[b - 1, :, 128:256] = high[:, piece]
                    win_lo[b - 1, :, 128:256] = low[:, piece]
        for b in range(0, 16, 4):
            wide = dot(win_hi[b : b + 4].reshape(512, 256), band_f[k])
            value = wide[:, :128] + wide[:, 128:]
            value = value + dot(win_lo[b : b + 4].reshape(512, 256), band_f[k, :, 0:128])
            for part in range(4):
                image[k, :, 128 * (b + part) : 128 * (b + part) + 128] = value[
                    128 * part : 128 * part + 128]

    def back_y(c):
        start = ORDER[c] * UNIT

        @pl.loop(0, VIEWS)
        def _(k):
            arrived(k, c)
            rows = slice(start, start + UNIT)
            ratio = arr[k, rows, :] / image[k, rows, :]
            high, low = split(pltpu.roll(ratio, 64, 1))
            for b in range(16):
                piece = slice(128 * b, 128 * b + 128)
                before = (b - 1) % 16
                bwin_hi[b, :, 0:128] = high[:, piece]
                bwin_lo[b, :, 0:128] = low[:, piece]
                bwin_hi[before, :, 128:256] = high[:, piece]
                bwin_lo[before, :, 128:256] = low[:, piece]
            wide = dot(bwin_hi[...].reshape(256, 256), band_b[k])
            value = wide[:, :128] + wide[:, 128:]
            value = value + dot(bwin_lo[...].reshape(256, 256), band_b[k, :, 0:128])
            high, low = split(value)
            into = slice((c % 2) * UNIT, (c % 2) * UNIT + UNIT)
            for b in range(16):
                spread_hi[k, into, 128 * b : 128 * b + 128] = high[16 * b : 16 * b + 16]
                spread_lo[k, into, 128 * b : 128 * b + 128] = low[16 * b : 16 * b + 16]

    def back_x(g):
        inner = g == GROUPS - 1
        base, count = (REACH, TILE) if inner else (0, 256)
        for start in range(0, COLS, 256):
            cols = slice(start, start + 256)
            high = spread_hi[:, :, cols].reshape(256, 256)
            low = spread_lo[:, :, cols].reshape(256, 256)
            value = dot(band_xt[g, base : base + count, :], high)
            value = value + dot(band_xt[g, 256 + base : 256 + base + count, :], high)
            value = value + dot(band_xt[g, base : base + count, :], low)
            if g == 0:
                acc[:, cols] = value
            else:
                acc[base : base + count, cols] += value

    def edge(side):
        if side == 0:
            return pltpu.make_async_remote_copy(
                acc.at[pl.ds(REACH + TILE, REACH)], edges.at[0],
                cs_sem.at[0], c_sem.at[0], device_id=(up, position), device_id_type=MESH)
        return pltpu.make_async_remote_copy(
            acc.at[pl.ds(0, REACH)], edges.at[1],
            cs_sem.at[1], c_sem.at[1], device_id=(down, position), device_id_type=MESH)

    for item in PLAN:
        if item[0] == "own":
            own(item[1])
        elif item[0] == "relay":
            relay(item[1], item[2])
        elif item[0] == "y":
            back_y(item[1])
        elif item[0] == "x":
            back_x(item[1])
        elif item[0] == "edge":
            edge(0).start()
            edge(1).start()
        else:
            pl.loop(item[1], item[2])(forward)
    edge(0).wait_recv()
    edge(1).wait_recv()
    count = jnp.broadcast_to(taps_ref[3 * VIEWS : 3 * VIEWS + 1, 0:128], (UNIT, 128))
    for part in range(TILE // UNIT):
        rows = slice(REACH + part * UNIT, REACH + part * UNIT + UNIT)
        total = acc[rows, :]
        if part < REACH // UNIT:
            total = total + edges[0, part * UNIT : part * UNIT + UNIT, :]
        if part >= (TILE - REACH) // UNIT:
            low_row = part * UNIT - (TILE - REACH)
            total = total + edges[1, low_row : low_row + UNIT, :]
        value = est[rows, :] * total
        for b in range(16):
            cols = slice(128 * b, 128 * b + 128)
            out_ref[0, part * UNIT : part * UNIT + UNIT, cols] = value[:, cols] / count

    halo(0).wait_send()
    halo(1).wait_send()
    edge(0).wait_send()
    edge(1).wait_send()
    for c in range(CHUNKS):
        for turn in range(2):
            for index in range(3):
                x_copy(index, turn, c).wait_send()
            for step in range(4):
                _, _, _, y2, _ = y_route(step, turn, c)

                @pl.when(y2 != y)
                def _():
                    y_copy(step, turn, c).wait_send()


def per_device(estimate, views, psf, offsets, lengths):
    f32, bf16 = jnp.float32, jnp.bfloat16
    anywhere = pl.BlockSpec(memory_space=pl.ANY)
    vmem = pl.BlockSpec(memory_space=pltpu.VMEM)
    smem = pl.BlockSpec(memory_space=pltpu.SMEM)
    dma = pltpu.SemaphoreType.DMA
    return pl.pallas_call(
        kernel,
        out_shape=jax.ShapeDtypeStruct(estimate.shape, f32),
        in_specs=[anywhere, anywhere, vmem, smem, smem],
        out_specs=vmem,
        scratch_shapes=[
            pltpu.VMEM((2 * VIEWS, TILE, COLS), f32),
            pltpu.VMEM((VIEWS, TILE, COLS), f32),
            pltpu.VMEM((256, COLS), f32),
            pltpu.VMEM((256, PADDED), bf16),
            pltpu.VMEM((256, PADDED), bf16),
            pltpu.VMEM((16, TILE, 256), bf16),
            pltpu.VMEM((16, TILE, 256), bf16),
            pltpu.VMEM((16, UNIT, 256), bf16),
            pltpu.VMEM((16, UNIT, 256), bf16),
            pltpu.VMEM((VIEWS, 2 * UNIT, COLS), bf16),
            pltpu.VMEM((VIEWS, 2 * UNIT, COLS), bf16),
            pltpu.VMEM((256, COLS), f32),
            pltpu.VMEM((2, REACH, COLS), f32),
            pltpu.VMEM((VIEWS, 2 * TILE, 256), bf16),
            pltpu.VMEM((GROUPS, 512, 256), bf16),
            pltpu.VMEM((VIEWS, 256, 256), bf16),
            pltpu.VMEM((VIEWS, 256, 256), bf16),
            pltpu.VMEM((VIEWS, TILE, 256), f32),
            pltpu.VMEM((4 * VIEWS, 256), f32),
            dma((3, 2, CHUNKS)),
            dma((4, 2, CHUNKS)),
            dma((2 * VIEWS, CHUNKS)),
            dma((2,)),
            dma((2,)),
            dma((2,)),
            dma((2,)),
            dma,
        ],
        compiler_params=pltpu.CompilerParams(
            collective_id=0, has_side_effects=True, vmem_limit_bytes=60 * 2**20
        ),
        name="deconvolve",
    )(estimate, views, psf, offsets, lengths)


def solution(mesh):
    return jax.shard_map(
        per_device,
        mesh=mesh,
        in_specs=(P("view", "joined", None), P("view", None, "joined", None), P(), P(), P()),
        out_specs=P("view", "joined", None),
        check_vma=False,
    )
```

```python
import jax
import jax.numpy as jnp
from jax import lax
from jax.experimental import pallas as pl
from jax.experimental.pallas import tpu as pltpu
from jax.sharding import PartitionSpec as P

MESH = pl.DeviceIdType.MESH
VIEWS = 8
BLOCKS = 2
ZB = 8
TAPS = 65
REACH = 48
TILE = 128
COLS = 2048
SPAN = TILE + 2 * REACH
PADDED = COLS + 128
UNIT = 16
ORDER = (0, 1, 2, 5, 6, 7, 3, 4)
CHUNKS = len(ORDER)
GROUPS = CHUNKS // 2
STEPS = (1, 3, 2)
AHEAD = 3
LAG = 2
SKEW = 1


def travel():
    turns = []
    for t in range(CHUNKS + SKEW):
        if t < CHUNKS:
            turns.append((t, (1, 3)))
        if t >= SKEW:
            turns.append((t - SKEW, (2,)))
    return turns


PACE = 2


def plan():
    pieces, last = [], {}
    for c, steps in TRAVEL:
        for turn in range(2):
            for step in steps:
                pieces.append(("relay", c, step, turn))
                last[c] = len(pieces) - 1
    work = [(3, ("estimate",))]
    work += [(4 + k, ("forward", k)) for k in range(VIEWS)]
    for c in range(CHUNKS):
        work += [(last[c] + LAG + near, ("y", c, near)) for near in range(4)]
        if c % 2:
            work += [(0, ("x", c // 2, half)) for half in range(2)]
            if c == CHUNKS - 3:
                work.append((0, ("edge",)))
    items = []
    for index, piece in enumerate(pieces):
        items.append(piece)
        c = piece[1] + AHEAD
        if piece[2:] == (3, 1) and c < CHUNKS:
            items.append(("own", c))
        for _ in range(PACE):
            if work and work[0][0] <= index:
                items.append(work.pop(0)[1])
    return items + [item for _, item in work]


TRAVEL = travel()
PLAN = plan()


def split(value):
    high = value.astype(jnp.bfloat16)
    low = (value - high.astype(jnp.float32)).astype(jnp.bfloat16)
    return high, low


def dot(a, b):
    return jnp.dot(a, b, preferred_element_type=jnp.float32)


def kernel(
    est_ref, views_ref, psf_ref, offsets_ref, lengths_ref, out_ref,
    arr, image, est, est_hi, est_lo, win_hi, win_lo, bwin_hi, bwin_lo,
    spread_hi, spread_lo, acc, edges, band_x, band_xt, band_f, band_b, rows_x, taps_ref,
    x_sem, y_sem, r_sem, e_sem, es_sem, c_sem, cs_sem, l_sem,
):
    tile = lax.axis_index("joined")
    position = lax.axis_index("view")
    y = position // 4
    x = position % 4
    tiles = 8
    up = lax.rem(tile + 1, tiles)
    down = lax.rem(tile + tiles - 1, tiles)

    barrier = pltpu.get_barrier_semaphore()
    peers = [(tile, y * 4 + (x + d) % 4) for d in (1, 2, 3)]
    peers += [(tile, ((y + d) % 4) * 4 + x) for d in (1, 2, 3)]
    peers += [(up, position), (down, position)]
    for peer in peers:
        pl.semaphore_signal(barrier, inc=1, device_id=peer, device_id_type=MESH)
    pl.semaphore_wait(barrier, len(peers))

    def halo(side):
        if side == 0:
            return pltpu.make_async_remote_copy(
                est_ref.at[0, pl.ds(TILE - REACH, REACH)], est.at[pl.ds(0, REACH)],
                es_sem.at[0], e_sem.at[0], device_id=(up, position), device_id_type=MESH)
        return pltpu.make_async_remote_copy(
            est_ref.at[0, pl.ds(0, REACH)], est.at[pl.ds(REACH + TILE, REACH)],
            es_sem.at[1], e_sem.at[1], device_id=(down, position), device_id_type=MESH)

    halo(0).start()
    halo(1).start()
    own_est = pltpu.make_async_copy(est_ref.at[0], est.at[pl.ds(REACH, TILE)], l_sem)
    own_est.start()

    def side_of(turn, source):
        home = jnp.where(source % 2 == y // 2, 1, 0)
        return (turn + y + home) % 2

    def x_copy(index, turn, c):
        rows = pl.ds(ORDER[c] * UNIT, UNIT)
        h = side_of(turn, x)
        x2 = (x + STEPS[index]) % 4
        y2 = BLOCKS * (x % 2) + h
        slot = jnp.where(y2 == y, 2 * y + x // 2, VIEWS + 2 * x + h)
        return pltpu.make_async_remote_copy(
            views_ref.at[0, 4 * h + x2, rows], arr.at[slot, rows],
            x_sem.at[index, turn, c], r_sem.at[slot, c],
            device_id=(tile, y * 4 + x2), device_id_type=MESH)

    def y_route(step, turn, c):
        xs = (x - step) % 4
        h = side_of(turn, xs)
        y2 = BLOCKS * (xs % 2) + h
        return pl.ds(ORDER[c] * UNIT, UNIT), h, xs, y2, 2 * y + xs // 2

    def y_copy(step, turn, c):
        rows, h, xs, y2, k = y_route(step, turn, c)
        source = views_ref.at[0, 4 * h + x, rows] if step == 0 else arr.at[VIEWS + 2 * xs + h, rows]
        return pltpu.make_async_remote_copy(
            source, arr.at[k, rows], y_sem.at[step, turn, c], r_sem.at[k, c],
            device_id=(tile, y2 * 4 + x), device_id_type=MESH)

    def arrived(slot, c):
        rows = pl.ds(ORDER[c] * UNIT, UNIT)
        pltpu.make_async_copy(
            views_ref.at[0, 0, rows], arr.at[slot, rows], r_sem.at[slot, c]).wait()

    def own(c):
        for turn in range(2):
            rows, h, _, y2, k = y_route(0, turn, c)

            @pl.when(y2 != y)
            def _():
                y_copy(0, turn, c).start()

            @pl.when(y2 == y)
            def _():
                pltpu.make_async_copy(
                    views_ref.at[0, 4 * h + x, rows], arr.at[k, rows], r_sem.at[k, c]).start()

    def relay(c, step, turn):
        _, h, xs, y2, _ = y_route(step, turn, c)

        @pl.when(y2 != y)
        def _():
            arrived(VIEWS + 2 * xs + h, c)
            y_copy(step, turn, c).start()

    for c, steps in TRAVEL:
        for index, step in enumerate(STEPS):
            if step in steps:
                for turn in range(2):
                    x_copy(index, turn, c).start()
    for c in range(AHEAD):
        own(c)

    block, plane_row = position // ZB, position % ZB
    blank = jnp.zeros((VIEWS, 128 - TAPS), jnp.float32)
    columns = []
    for axis in range(2):
        taps = psf_ref[:, axis, :]
        taps = taps / jnp.sum(taps, axis=1, keepdims=True)
        columns.append(jnp.transpose(jnp.concatenate([taps, blank], axis=1)))
    tap = lax.broadcasted_iota(jnp.int32, (128, 256), 0)
    lane = lax.broadcasted_iota(jnp.int32, (128, 256), 1)
    total = jnp.zeros((VIEWS, 256), jnp.float32)
    for k in range(VIEWS):
        live = jnp.where(plane_row < lengths_ref[block, k], 1.0, 0.0)
        total = total + live
        dx, dy = offsets_ref[0, k], offsets_ref[1, k]
        places = ((0, lane - 16 - dx), (1, 224 - lane - dy), (1, lane - 160 - dy))
        for kind, (axis, place) in enumerate(places):
            column = jnp.broadcast_to(columns[axis][:, k : k + 1], (128, 256))
            line = jnp.sum(jnp.where(place == tap, column, 0.0), axis=0, keepdims=True)
            if kind == 2:
                line = line * live
            taps_ref[kind * VIEWS + k : kind * VIEWS + k + 1, :] = line
    taps_ref[3 * VIEWS : 4 * VIEWS, :] = total

    @pl.loop(0, VIEWS)
    def _(k):
        row = jnp.broadcast_to(taps_ref[pl.ds(k, 1), :], (TILE, 256))
        band = pltpu.roll(row, 0, 1, stride=1, stride_axis=0)
        rows_x[k] = band
        high, low = split(band)
        band_x[k, 0:TILE, :] = high
        band_x[k, TILE : 2 * TILE, :] = low
        for first, target in ((VIEWS, band_f), (2 * VIEWS, band_b)):
            row = jnp.broadcast_to(taps_ref[pl.ds(first + k, 1), :], (256, 256))
            band = pltpu.roll(row, 0, 1, stride=1, stride_axis=0)[:, :128]
            high, low = split(band)
            target[k, :, 0:128] = high
            target[k, :, 128:256] = low

    for g in range(GROUPS):
        first, second = ORDER[2 * g] * UNIT, ORDER[2 * g + 1] * UNIT
        picked = jnp.concatenate(
            [rows_x[:, first : first + UNIT, :], rows_x[:, second : second + UNIT, :]], axis=1)
        band = jnp.transpose(picked.reshape(256, 256))
        high, low = split(band)
        if g < GROUPS - 1:
            band_xt[g, 0:256, :] = high
            band_xt[g, 256:512, :] = low
        else:
            band_xt[g, 0:TILE, :] = high[REACH : REACH + TILE]
            band_xt[g, TILE : 2 * TILE, :] = low[REACH : REACH + TILE]

    def estimate():
        own_est.wait()
        halo(0).wait_recv()
        halo(1).wait_recv()
        est[SPAN:256, :] = jnp.zeros((256 - SPAN, COLS), jnp.float32)

        @pl.loop(0, 256 // 32)
        def _(i):
            rows = pl.ds(pl.multiple_of(i * 32, 32), 32)
            high, low = split(pltpu.roll(est[rows, :], 64, 1))
            est_hi[rows, 0:COLS] = high
            est_lo[rows, 0:COLS] = low
            est_hi[rows, COLS:PADDED] = high[:, 0:128]
            est_lo[rows, COLS:PADDED] = low[:, 0:128]

        count = jnp.broadcast_to(taps_ref[3 * VIEWS : 3 * VIEWS + 1, 0:1], (TILE, 1))
        est[REACH : REACH + TILE, :] = est[REACH : REACH + TILE, :] / count

    def forward(k):
        for first in range(0, PADDED, 256):
            width = min(256, PADDED - first)
            cols = pl.ds(first, width)
            wide = dot(band_x[k], est_hi[:, cols])
            value = wide[:TILE] + wide[TILE:] + dot(band_x[k, 0:TILE, :], est_lo[:, cols])
            high, low = split(value)
            for part in range(width // 128):
                b = first // 128 + part
                piece = slice(128 * part, 128 * part + 128)
                if b < 16:
                    win_hi[b, :, 0:128] = high[:, piece]
                    win_lo[b, :, 0:128] = low[:, piece]
                if b > 0:
                    win_hi[b - 1, :, 128:256] = high[:, piece]
                    win_lo[b - 1, :, 128:256] = low[:, piece]
        for b in range(0, 16, 4):
            wide = dot(win_hi[b : b + 4].reshape(512, 256), band_f[k])
            value = wide[:, :128] + wide[:, 128:]
            value = value + dot(win_lo[b : b + 4].reshape(512, 256), band_f[k, :, 0:128])
            for part in range(4):
                image[k, :, 128 * (b + part) : 128 * (b + part) + 128] = value[
                    128 * part : 128 * part + 128]

    def back_y(c, near):
        start = ORDER[c] * UNIT

        far = (0, 1, 3, 2)[near]

        @pl.loop(0, 2)
        def _(turn):
            k = 2 * ((y + far) % 4) + turn
            arrived(k, c)
            rows = slice(start, start + UNIT)
            ratio = arr[k, rows, :] / image[k, rows, :]
            high, low = split(pltpu.roll(ratio, 64, 1))
            for b in range(16):
                piece = slice(128 * b, 128 * b + 128)
                before = (b - 1) % 16
                bwin_hi[b, :, 0:128] = high[:, piece]
                bwin_lo[b, :, 0:128] = low[:, piece]
                bwin_hi[before, :, 128:256] = high[:, piece]
                bwin_lo[before, :, 128:256] = low[:, piece]
            wide = dot(bwin_hi[...].reshape(256, 256), band_b[k])
            value = wide[:, :128] + wide[:, 128:]
            value = value + dot(bwin_lo[...].reshape(256, 256), band_b[k, :, 0:128])
            high, low = split(value)
            into = slice((c % 2) * UNIT, (c % 2) * UNIT + UNIT)
            for b in range(16):
                spread_hi[k, into, 128 * b : 128 * b + 128] = high[16 * b : 16 * b + 16]
                spread_lo[k, into, 128 * b : 128 * b + 128] = low[16 * b : 16 * b + 16]

    def back_x(g, half):
        for start in range(half * COLS // 2, (half + 1) * COLS // 2, 256):
            cols = slice(start, start + 256)
            high = spread_hi[:, :, cols].reshape(256, 256)
            low = spread_lo[:, :, cols].reshape(256, 256)
            wide = dot(band_xt[g], high)
            value = wide[:256] + wide[256:] + dot(band_xt[g, 0:256, :], low)
            if g == 0:
                acc[:, cols] = value
            else:
                acc[:, cols] += value

    def last_x(half):
        g = GROUPS - 1
        for start in range(half * COLS // 2, (half + 1) * COLS // 2, 256):
            cols = slice(start, start + 256)
            high = spread_hi[:, :, cols].reshape(256, 256)
            low = spread_lo[:, :, cols].reshape(256, 256)
            wide = dot(band_xt[g, 0 : 2 * TILE, :], high)
            value = wide[:TILE] + wide[TILE:] + dot(band_xt[g, 0:TILE, :], low)
            value = value + acc[REACH : REACH + TILE, cols]
            value = value * est[REACH : REACH + TILE, cols]
            out_ref[0, :, cols] = value

    def edge(side):
        if side == 0:
            return pltpu.make_async_remote_copy(
                acc.at[pl.ds(REACH + TILE, REACH)], edges.at[0],
                cs_sem.at[0], c_sem.at[0], device_id=(up, position), device_id_type=MESH)
        return pltpu.make_async_remote_copy(
            acc.at[pl.ds(0, REACH)], edges.at[1],
            cs_sem.at[1], c_sem.at[1], device_id=(down, position), device_id_type=MESH)

    def sent(c):
        for turn in range(2):
            for index in range(3):
                x_copy(index, turn, c).wait_send()
            for step in range(4):
                _, _, _, y2, _ = y_route(step, turn, c)

                @pl.when(y2 != y)
                def _():
                    y_copy(step, turn, c).wait_send()

    for item in PLAN:
        if item[0] == "own":
            own(item[1])
        elif item[0] == "relay":
            relay(*item[1:])
        elif item[0] == "estimate":
            estimate()
        elif item[0] == "forward":
            forward(item[1])
        elif item[0] == "y":
            if item[1:] == (CHUNKS - 1, 0):
                halo(0).wait_send()
                halo(1).wait_send()
                for c in range(CHUNKS - 4):
                    sent(c)
            if item[1:] == (CHUNKS - 1, 3):
                edge(0).wait_recv()
                edge(1).wait_recv()
                acc[REACH : 2 * REACH, :] += edges[0]
                acc[TILE : REACH + TILE, :] += edges[1]
            back_y(*item[1:])
        elif item[0] == "edge":
            edge(0).start()
            edge(1).start()
        elif item[1] < GROUPS - 1:
            back_x(*item[1:])
        else:
            last_x(item[2])

    edge(0).wait_send()
    edge(1).wait_send()
    for c in range(CHUNKS - 4, CHUNKS):
        sent(c)


def per_device(estimate, views, psf, offsets, lengths):
    f32, bf16 = jnp.float32, jnp.bfloat16
    anywhere = pl.BlockSpec(memory_space=pl.ANY)
    vmem = pl.BlockSpec(memory_space=pltpu.VMEM)
    smem = pl.BlockSpec(memory_space=pltpu.SMEM)
    dma = pltpu.SemaphoreType.DMA
    return pl.pallas_call(
        kernel,
        out_shape=jax.ShapeDtypeStruct(estimate.shape, f32),
        in_specs=[anywhere, anywhere, vmem, smem, smem],
        out_specs=vmem,
        scratch_shapes=[
            pltpu.VMEM((2 * VIEWS, TILE, COLS), f32),
            pltpu.VMEM((VIEWS, TILE, COLS), f32),
            pltpu.VMEM((256, COLS), f32),
            pltpu.VMEM((256, PADDED), bf16),
            pltpu.VMEM((256, PADDED), bf16),
            pltpu.VMEM((16, TILE, 256), bf16),
            pltpu.VMEM((16, TILE, 256), bf16),
            pltpu.VMEM((16, UNIT, 256), bf16),
            pltpu.VMEM((16, UNIT, 256), bf16),
            pltpu.VMEM((VIEWS, 2 * UNIT, COLS), bf16),
            pltpu.VMEM((VIEWS, 2 * UNIT, COLS), bf16),
            pltpu.VMEM((256, COLS), f32),
            pltpu.VMEM((2, REACH, COLS), f32),
            pltpu.VMEM((VIEWS, 2 * TILE, 256), bf16),
            pltpu.VMEM((GROUPS, 512, 256), bf16),
            pltpu.VMEM((VIEWS, 256, 256), bf16),
            pltpu.VMEM((VIEWS, 256, 256), bf16),
            pltpu.VMEM((VIEWS, TILE, 256), f32),
            pltpu.VMEM((4 * VIEWS, 256), f32),
            dma((3, 2, CHUNKS)),
            dma((4, 2, CHUNKS)),
            dma((2 * VIEWS, CHUNKS)),
            dma((2,)),
            dma((2,)),
            dma((2,)),
            dma((2,)),
            dma,
        ],
        compiler_params=pltpu.CompilerParams(
            collective_id=0, has_side_effects=True, vmem_limit_bytes=60 * 2**20
        ),
        name="deconvolve",
    )(estimate, views, psf, offsets.T, lengths.T)


def solution(mesh):
    return jax.shard_map(
        per_device,
        mesh=mesh,
        in_specs=(P("view", "joined", None), P("view", None, "joined", None), P(), P(), P()),
        out_specs=P("view", "joined", None),
        check_vma=False,
    )
```

```python
import jax
import jax.numpy as jnp
from jax import lax
from jax.experimental import pallas as pl
from jax.experimental.pallas import tpu as pltpu
from jax.sharding import PartitionSpec as P

MESH = pl.DeviceIdType.MESH
VIEWS = 8
BLOCKS = 2
ZB = 8
TAPS = 65
REACH = 48
TILE = 128
COLS = 2048
SPAN = TILE + 2 * REACH
PADDED = COLS + 128
UNIT = 16
ORDER = (0, 1, 2, 5, 6, 7, 3, 4)
CHUNKS = len(ORDER)
GROUPS = CHUNKS // 2
STEPS = (1, 3, 2)
AHEAD = 3
LAG = 3
SKEW = 1


def travel():
    turns = []
    for t in range(CHUNKS + SKEW):
        if t < CHUNKS:
            turns.append((t, (1, 3)))
        if t >= SKEW:
            turns.append((t - SKEW, (2,)))
    return turns


PACE = 2


def plan():
    pieces, last = [], {}
    for c, steps in TRAVEL:
        for turn in range(2):
            for step in steps:
                pieces.append(("relay", c, step, turn))
                last[c] = len(pieces) - 1
    work = [(3, ("estimate",))]
    work += [(4 + k, ("forward", k)) for k in range(VIEWS)]
    for c in range(CHUNKS):
        work += [(last[c] + LAG + near, ("y", c, near)) for near in range(4)]
        if c % 2:
            work += [(0, ("x", c // 2, half)) for half in range(2)]
            if c == CHUNKS - 3:
                work.append((0, ("edge",)))
    items = []
    for index, piece in enumerate(pieces):
        items.append(piece)
        c = piece[1] + AHEAD
        if piece[2:] == (3, 1) and c < CHUNKS:
            items.append(("own", c))
        for _ in range(PACE):
            if work and work[0][0] <= index:
                items.append(work.pop(0)[1])
    return items + [item for _, item in work]


TRAVEL = travel()
PLAN = plan()


def split(value):
    high = value.astype(jnp.bfloat16)
    low = (value - high.astype(jnp.float32)).astype(jnp.bfloat16)
    return high, low


def dot(a, b):
    return jnp.dot(a, b, preferred_element_type=jnp.float32)


def kernel(
    est_ref, views_ref, psf_ref, offsets_ref, lengths_ref, out_ref,
    arr, image, est, est_hi, est_lo, win_hi, win_lo, bwin_hi, bwin_lo,
    spread_hi, spread_lo, acc, edges, band_x, band_xt, band_f, band_b, rows_x, taps_ref,
    x_sem, y_sem, r_sem, e_sem, es_sem, c_sem, cs_sem, l_sem,
):
    tile = lax.axis_index("joined")
    position = lax.axis_index("view")
    y = position // 4
    x = position % 4
    tiles = 8
    up = lax.rem(tile + 1, tiles)
    down = lax.rem(tile + tiles - 1, tiles)

    barrier = pltpu.get_barrier_semaphore()
    peers = [(tile, y * 4 + (x + d) % 4) for d in (1, 2, 3)]
    peers += [(tile, ((y + d) % 4) * 4 + x) for d in (1, 2, 3)]
    peers += [(up, position), (down, position)]
    for peer in peers:
        pl.semaphore_signal(barrier, inc=1, device_id=peer, device_id_type=MESH)
    pl.semaphore_wait(barrier, len(peers))

    def halo(side):
        if side == 0:
            return pltpu.make_async_remote_copy(
                est_ref.at[0, pl.ds(TILE - REACH, REACH)], est.at[pl.ds(0, REACH)],
                es_sem.at[0], e_sem.at[0], device_id=(up, position), device_id_type=MESH)
        return pltpu.make_async_remote_copy(
            est_ref.at[0, pl.ds(0, REACH)], est.at[pl.ds(REACH + TILE, REACH)],
            es_sem.at[1], e_sem.at[1], device_id=(down, position), device_id_type=MESH)

    own_est = pltpu.make_async_copy(est_ref.at[0], est.at[pl.ds(REACH, TILE)], l_sem)

    def side_of(turn, source):
        home = jnp.where(source % 2 == y // 2, 1, 0)
        return (turn + y + home) % 2

    def x_copy(index, turn, c):
        rows = pl.ds(ORDER[c] * UNIT, UNIT)
        h = side_of(turn, x)
        x2 = (x + STEPS[index]) % 4
        y2 = BLOCKS * (x % 2) + h
        slot = jnp.where(y2 == y, 2 * y + x // 2, VIEWS + 2 * x + h)
        return pltpu.make_async_remote_copy(
            views_ref.at[0, 4 * h + x2, rows], arr.at[slot, rows],
            x_sem.at[index, turn, c], r_sem.at[slot, c],
            device_id=(tile, y * 4 + x2), device_id_type=MESH)

    def y_route(step, turn, c):
        xs = (x - step) % 4
        h = side_of(turn, xs)
        y2 = BLOCKS * (xs % 2) + h
        return pl.ds(ORDER[c] * UNIT, UNIT), h, xs, y2, 2 * y + xs // 2

    def y_copy(step, turn, c):
        rows, h, xs, y2, k = y_route(step, turn, c)
        source = views_ref.at[0, 4 * h + x, rows] if step == 0 else arr.at[VIEWS + 2 * xs + h, rows]
        return pltpu.make_async_remote_copy(
            source, arr.at[k, rows], y_sem.at[step, turn, c], r_sem.at[k, c],
            device_id=(tile, y2 * 4 + x), device_id_type=MESH)

    def arrived(slot, c):
        rows = pl.ds(ORDER[c] * UNIT, UNIT)
        pltpu.make_async_copy(
            views_ref.at[0, 0, rows], arr.at[slot, rows], r_sem.at[slot, c]).wait()

    def own(c):
        for turn in range(2):
            rows, h, _, y2, k = y_route(0, turn, c)

            @pl.when(y2 != y)
            def _():
                y_copy(0, turn, c).start()

            @pl.when(y2 == y)
            def _():
                pltpu.make_async_copy(
                    views_ref.at[0, 4 * h + x, rows], arr.at[k, rows], r_sem.at[k, c]).start()

    def relay(c, step, turn):
        _, h, xs, y2, _ = y_route(step, turn, c)

        @pl.when(y2 != y)
        def _():
            arrived(VIEWS + 2 * xs + h, c)
            y_copy(step, turn, c).start()

    def depart(travel):
        for c, steps in travel:
            for turn in range(2):
                for index, step in enumerate(STEPS):
                    if step in steps:
                        x_copy(index, turn, c).start()

    depart(TRAVEL[:1])
    own(0)
    halo(0).start()
    halo(1).start()
    own_est.start()
    depart(TRAVEL[1:2])
    for c in range(1, AHEAD):
        own(c)
    depart(TRAVEL[2:])

    block, plane_row = position // ZB, position % ZB
    blank = jnp.zeros((VIEWS, 128 - TAPS), jnp.float32)
    columns = []
    for axis in range(2):
        taps = psf_ref[:, axis, :]
        taps = taps / jnp.sum(taps, axis=1, keepdims=True)
        columns.append(jnp.transpose(jnp.concatenate([taps, blank], axis=1)))
    tap = lax.broadcasted_iota(jnp.int32, (128, 256), 0)
    lane = lax.broadcasted_iota(jnp.int32, (128, 256), 1)
    total = jnp.zeros((VIEWS, 256), jnp.float32)
    for k in range(VIEWS):
        live = jnp.where(plane_row < lengths_ref[block, k], 1.0, 0.0)
        total = total + live
        dx, dy = offsets_ref[0, k], offsets_ref[1, k]
        places = ((0, lane - 16 - dx), (1, 224 - lane - dy), (1, lane - 160 - dy))
        for kind, (axis, place) in enumerate(places):
            column = jnp.broadcast_to(columns[axis][:, k : k + 1], (128, 256))
            line = jnp.sum(jnp.where(place == tap, column, 0.0), axis=0, keepdims=True)
            if kind == 2:
                line = line * live
            taps_ref[kind * VIEWS + k : kind * VIEWS + k + 1, :] = line
    taps_ref[3 * VIEWS : 4 * VIEWS, :] = total

    @pl.loop(0, VIEWS)
    def _(k):
        row = jnp.broadcast_to(taps_ref[pl.ds(k, 1), :], (TILE, 256))
        band = pltpu.roll(row, 0, 1, stride=1, stride_axis=0)
        rows_x[k] = band
        high, low = split(band)
        band_x[k, 0:TILE, :] = high
        band_x[k, TILE : 2 * TILE, :] = low
        for first, target in ((VIEWS, band_f), (2 * VIEWS, band_b)):
            row = jnp.broadcast_to(taps_ref[pl.ds(first + k, 1), :], (256, 256))
            band = pltpu.roll(row, 0, 1, stride=1, stride_axis=0)[:, :128]
            high, low = split(band)
            target[k, :, 0:128] = high
            target[k, :, 128:256] = low

    for g in range(GROUPS):
        first, second = ORDER[2 * g] * UNIT, ORDER[2 * g + 1] * UNIT
        picked = jnp.concatenate(
            [rows_x[:, first : first + UNIT, :], rows_x[:, second : second + UNIT, :]], axis=1)
        band = jnp.transpose(picked.reshape(256, 256))
        high, low = split(band)
        if g < GROUPS - 1:
            band_xt[g, 0:256, :] = high
            band_xt[g, 256:512, :] = low
        else:
            band_xt[g, 0:TILE, :] = high[REACH : REACH + TILE]
            band_xt[g, TILE : 2 * TILE, :] = low[REACH : REACH + TILE]

    def estimate():
        own_est.wait()
        halo(0).wait_recv()
        halo(1).wait_recv()
        est[SPAN:256, :] = jnp.zeros((256 - SPAN, COLS), jnp.float32)

        @pl.loop(0, 256 // 32)
        def _(i):
            rows = pl.ds(pl.multiple_of(i * 32, 32), 32)
            high, low = split(pltpu.roll(est[rows, :], 64, 1))
            est_hi[rows, 0:COLS] = high
            est_lo[rows, 0:COLS] = low
            est_hi[rows, COLS:PADDED] = high[:, 0:128]
            est_lo[rows, COLS:PADDED] = low[:, 0:128]

        count = jnp.broadcast_to(taps_ref[3 * VIEWS : 3 * VIEWS + 1, 0:1], (TILE, 1))
        est[REACH : REACH + TILE, :] = est[REACH : REACH + TILE, :] / count

    def forward(k):
        for first in range(0, PADDED, 256):
            width = min(256, PADDED - first)
            cols = pl.ds(first, width)
            wide = dot(band_x[k], est_hi[:, cols])
            value = wide[:TILE] + wide[TILE:] + dot(band_x[k, 0:TILE, :], est_lo[:, cols])
            high, low = split(value)
            for part in range(width // 128):
                b = first // 128 + part
                piece = slice(128 * part, 128 * part + 128)
                if b < 16:
                    win_hi[b, :, 0:128] = high[:, piece]
                    win_lo[b, :, 0:128] = low[:, piece]
                if b > 0:
                    win_hi[b - 1, :, 128:256] = high[:, piece]
                    win_lo[b - 1, :, 128:256] = low[:, piece]
        for b in range(0, 16, 4):
            wide = dot(win_hi[b : b + 4].reshape(512, 256), band_f[k])
            value = wide[:, :128] + wide[:, 128:]
            value = value + dot(win_lo[b : b + 4].reshape(512, 256), band_f[k, :, 0:128])
            for part in range(4):
                image[k, :, 128 * (b + part) : 128 * (b + part) + 128] = value[
                    128 * part : 128 * part + 128]

    def back_y(c, near):
        start = ORDER[c] * UNIT

        far = (0, 1, 3, 2)[near]

        @pl.loop(0, 2)
        def _(turn):
            k = 2 * ((y + far) % 4) + turn
            arrived(k, c)
            rows = slice(start, start + UNIT)
            ratio = arr[k, rows, :] / image[k, rows, :]
            high, low = split(pltpu.roll(ratio, 64, 1))
            for b in range(16):
                piece = slice(128 * b, 128 * b + 128)
                before = (b - 1) % 16
                bwin_hi[b, :, 0:128] = high[:, piece]
                bwin_lo[b, :, 0:128] = low[:, piece]
                bwin_hi[before, :, 128:256] = high[:, piece]
                bwin_lo[before, :, 128:256] = low[:, piece]
            wide = dot(bwin_hi[...].reshape(256, 256), band_b[k])
            value = wide[:, :128] + wide[:, 128:]
            value = value + dot(bwin_lo[...].reshape(256, 256), band_b[k, :, 0:128])
            high, low = split(value)
            into = slice((c % 2) * UNIT, (c % 2) * UNIT + UNIT)
            for b in range(16):
                spread_hi[k, into, 128 * b : 128 * b + 128] = high[16 * b : 16 * b + 16]
                spread_lo[k, into, 128 * b : 128 * b + 128] = low[16 * b : 16 * b + 16]

    def back_x(g, half):
        for start in range(half * COLS // 2, (half + 1) * COLS // 2, 256):
            cols = slice(start, start + 256)
            high = spread_hi[:, :, cols].reshape(256, 256)
            low = spread_lo[:, :, cols].reshape(256, 256)
            wide = dot(band_xt[g], high)
            value = wide[:256] + wide[256:] + dot(band_xt[g, 0:256, :], low)
            if g == 0:
                acc[:, cols] = value
            else:
                acc[:, cols] += value

    def last_x(half):
        g = GROUPS - 1
        for start in range(half * COLS // 2, (half + 1) * COLS // 2, 256):
            cols = slice(start, start + 256)
            high = spread_hi[:, :, cols].reshape(256, 256)
            low = spread_lo[:, :, cols].reshape(256, 256)
            wide = dot(band_xt[g, 0 : 2 * TILE, :], high)
            value = wide[:TILE] + wide[TILE:] + dot(band_xt[g, 0:TILE, :], low)
            value = value + acc[REACH : REACH + TILE, cols]
            value = value * est[REACH : REACH + TILE, cols]
            out_ref[0, :, cols] = value

    def edge(side):
        if side == 0:
            return pltpu.make_async_remote_copy(
                acc.at[pl.ds(REACH + TILE, REACH)], edges.at[0],
                cs_sem.at[0], c_sem.at[0], device_id=(up, position), device_id_type=MESH)
        return pltpu.make_async_remote_copy(
            acc.at[pl.ds(0, REACH)], edges.at[1],
            cs_sem.at[1], c_sem.at[1], device_id=(down, position), device_id_type=MESH)

    def sent(c):
        for turn in range(2):
            for index in range(3):
                x_copy(index, turn, c).wait_send()
            for step in range(4):
                _, _, _, y2, _ = y_route(step, turn, c)

                @pl.when(y2 != y)
                def _():
                    y_copy(step, turn, c).wait_send()

    for item in PLAN:
        if item[0] == "own":
            own(item[1])
        elif item[0] == "relay":
            relay(*item[1:])
        elif item[0] == "estimate":
            estimate()
        elif item[0] == "forward":
            forward(item[1])
        elif item[0] == "y":
            if item[1:] == (CHUNKS - 1, 0):
                halo(0).wait_send()
                halo(1).wait_send()
                for c in range(CHUNKS - 4):
                    sent(c)
            if item[1:] == (CHUNKS - 1, 3):
                edge(0).wait_recv()
                edge(1).wait_recv()
                acc[REACH : 2 * REACH, :] += edges[0]
                acc[TILE : REACH + TILE, :] += edges[1]
            back_y(*item[1:])
        elif item[0] == "edge":
            edge(0).start()
            edge(1).start()
        elif item[1] < GROUPS - 1:
            back_x(*item[1:])
        else:
            last_x(item[2])

    edge(0).wait_send()
    edge(1).wait_send()
    for c in range(CHUNKS - 4, CHUNKS):
        sent(c)


def per_device(estimate, views, psf, offsets, lengths):
    operands = (estimate, views, psf, offsets.T, lengths.T)
    f32, bf16 = jnp.float32, jnp.bfloat16
    anywhere = pl.BlockSpec(memory_space=pl.ANY)
    vmem = pl.BlockSpec(memory_space=pltpu.VMEM)
    smem = pl.BlockSpec(memory_space=pltpu.SMEM)
    dma = pltpu.SemaphoreType.DMA
    return pl.pallas_call(
        kernel,
        out_shape=jax.ShapeDtypeStruct(estimate.shape, f32),
        in_specs=[anywhere, anywhere, vmem, smem, smem],
        out_specs=vmem,
        scratch_shapes=[
            pltpu.VMEM((2 * VIEWS, TILE, COLS), f32),
            pltpu.VMEM((VIEWS, TILE, COLS), f32),
            pltpu.VMEM((256, COLS), f32),
            pltpu.VMEM((256, PADDED), bf16),
            pltpu.VMEM((256, PADDED), bf16),
            pltpu.VMEM((16, TILE, 256), bf16),
            pltpu.VMEM((16, TILE, 256), bf16),
            pltpu.VMEM((16, UNIT, 256), bf16),
            pltpu.VMEM((16, UNIT, 256), bf16),
            pltpu.VMEM((VIEWS, 2 * UNIT, COLS), bf16),
            pltpu.VMEM((VIEWS, 2 * UNIT, COLS), bf16),
            pltpu.VMEM((256, COLS), f32),
            pltpu.VMEM((2, REACH, COLS), f32),
            pltpu.VMEM((VIEWS, 2 * TILE, 256), bf16),
            pltpu.VMEM((GROUPS, 512, 256), bf16),
            pltpu.VMEM((VIEWS, 256, 256), bf16),
            pltpu.VMEM((VIEWS, 256, 256), bf16),
            pltpu.VMEM((VIEWS, TILE, 256), f32),
            pltpu.VMEM((4 * VIEWS, 256), f32),
            dma((3, 2, CHUNKS)),
            dma((4, 2, CHUNKS)),
            dma((2 * VIEWS, CHUNKS)),
            dma((2,)),
            dma((2,)),
            dma((2,)),
            dma((2,)),
            dma,
        ],
        compiler_params=pltpu.CompilerParams(
            collective_id=0, has_side_effects=True, vmem_limit_bytes=50 * 2**20
        ),
        name="deconvolve",
    )(*(pltpu.with_memory_space_constraint(a, pltpu.HBM) for a in operands))


def solution(mesh):
    return jax.shard_map(
        per_device,
        mesh=mesh,
        in_specs=(P("view", "joined", None), P("view", None, "joined", None), P(), P(), P()),
        out_specs=P("view", "joined", None),
        check_vma=False,
    )
```

```python
import jax
import jax.numpy as jnp
from jax import lax
from jax.experimental import pallas as pl
from jax.experimental.pallas import tpu as pltpu
from jax.sharding import PartitionSpec as P

MESH = pl.DeviceIdType.MESH
VIEWS = 8
BLOCKS = 2
ZB = 8
TAPS = 65
REACH = 48
TILE = 128
COLS = 2048
SPAN = TILE + 2 * REACH
PADDED = COLS + 128
UNIT = 16
ORDER = (0, 1, 2, 5, 6, 7, 3, 4)
CHUNKS = len(ORDER)
GROUPS = CHUNKS // 2
STEPS = (1, 3, 2)
AHEAD = 3
LAG = 3
SKEW = 1


def travel():
    turns = []
    for t in range(CHUNKS + SKEW):
        if t < CHUNKS:
            turns.append((t, (1, 3)))
        if t >= SKEW:
            turns.append((t - SKEW, (2,)))
    return turns


PACE = 2


def plan():
    pieces, last = [], {}
    for c, steps in TRAVEL:
        for turn in range(2):
            for step in steps:
                pieces.append(("relay", c, step, turn))
                last[c] = len(pieces) - 1
    work = [(3, ("estimate",))]
    work += [(4 + k, ("forward", k)) for k in range(VIEWS)]
    for c in range(CHUNKS):
        work += [(last[c] + LAG + near, ("y", c, near)) for near in range(4)]
        if c % 2:
            work += [(0, ("x", c // 2, half)) for half in range(2)]
            if c == CHUNKS - 3:
                work.append((0, ("edge",)))
    items = []
    for index, piece in enumerate(pieces):
        items.append(piece)
        c = piece[1] + AHEAD
        if piece[2:] == (3, 1) and c < CHUNKS:
            items.append(("own", c))
        for _ in range(PACE):
            if work and work[0][0] <= index:
                items.append(work.pop(0)[1])
    return items + [item for _, item in work]


TRAVEL = travel()
PLAN = plan()


def split(value):
    high = value.astype(jnp.bfloat16)
    low = (value - high.astype(jnp.float32)).astype(jnp.bfloat16)
    return high, low


def dot(a, b):
    return jnp.dot(a, b, preferred_element_type=jnp.float32)


def kernel(
    est_ref, views_ref, psf_ref, offsets_ref, lengths_ref, out_ref,
    arr, image, est, est_hi, est_lo, win_hi, win_lo, bwin_hi, bwin_lo,
    spread_hi, spread_lo, acc, edges, band_x, band_xt, band_f, band_b, rows_x, taps_ref,
    x_sem, y_sem, r_sem, e_sem, es_sem, c_sem, cs_sem, l_sem,
):
    tile = lax.axis_index("joined")
    position = lax.axis_index("view")
    y = position // 4
    x = position % 4
    tiles = 8
    up = lax.rem(tile + 1, tiles)
    down = lax.rem(tile + tiles - 1, tiles)

    barrier = pltpu.get_barrier_semaphore()
    peers = [(tile, y * 4 + (x + d) % 4) for d in (1, 2, 3)]
    peers += [(tile, ((y + d) % 4) * 4 + x) for d in (1, 2, 3)]
    peers += [(up, position), (down, position)]
    for peer in peers:
        pl.semaphore_signal(barrier, inc=1, device_id=peer, device_id_type=MESH)
    pl.semaphore_wait(barrier, len(peers))

    def halo(side):
        if side == 0:
            return pltpu.make_async_remote_copy(
                est_ref.at[0, pl.ds(TILE - REACH, REACH)], est.at[pl.ds(0, REACH)],
                es_sem.at[0], e_sem.at[0], device_id=(up, position), device_id_type=MESH)
        return pltpu.make_async_remote_copy(
            est_ref.at[0, pl.ds(0, REACH)], est.at[pl.ds(REACH + TILE, REACH)],
            es_sem.at[1], e_sem.at[1], device_id=(down, position), device_id_type=MESH)

    own_est = pltpu.make_async_copy(est_ref.at[0], est.at[pl.ds(REACH, TILE)], l_sem)

    def side_of(turn, source):
        home = jnp.where(source % 2 == y // 2, 1, 0)
        return (turn + y + home) % 2

    def x_copy(index, turn, c):
        rows = pl.ds(ORDER[c] * UNIT, UNIT)
        h = side_of(turn, x)
        x2 = (x + STEPS[index]) % 4
        y2 = BLOCKS * (x % 2) + h
        slot = jnp.where(y2 == y, 2 * y + x // 2, VIEWS + 2 * x + h)
        return pltpu.make_async_remote_copy(
            views_ref.at[0, 4 * h + x2, rows], arr.at[slot, rows],
            x_sem.at[index, turn, c], r_sem.at[slot, c],
            device_id=(tile, y * 4 + x2), device_id_type=MESH)

    def y_route(step, turn, c):
        xs = (x - step) % 4
        h = side_of(turn, xs)
        y2 = BLOCKS * (xs % 2) + h
        return pl.ds(ORDER[c] * UNIT, UNIT), h, xs, y2, 2 * y + xs // 2

    def y_copy(step, turn, c):
        rows, h, xs, y2, k = y_route(step, turn, c)
        source = views_ref.at[0, 4 * h + x, rows] if step == 0 else arr.at[VIEWS + 2 * xs + h, rows]
        return pltpu.make_async_remote_copy(
            source, arr.at[k, rows], y_sem.at[step, turn, c], r_sem.at[k, c],
            device_id=(tile, y2 * 4 + x), device_id_type=MESH)

    def arrived(slot, c):
        rows = pl.ds(ORDER[c] * UNIT, UNIT)
        pltpu.make_async_copy(
            views_ref.at[0, 0, rows], arr.at[slot, rows], r_sem.at[slot, c]).wait()

    def own(c):
        for turn in range(2):
            rows, h, _, y2, k = y_route(0, turn, c)

            @pl.when(y2 != y)
            def _():
                y_copy(0, turn, c).start()

            @pl.when(y2 == y)
            def _():
                pltpu.make_async_copy(
                    views_ref.at[0, 4 * h + x, rows], arr.at[k, rows], r_sem.at[k, c]).start()

    def relay(c, step, turn):
        _, h, xs, y2, _ = y_route(step, turn, c)

        @pl.when(y2 != y)
        def _():
            arrived(VIEWS + 2 * xs + h, c)
            y_copy(step, turn, c).start()

    def depart(travel):
        for c, steps in travel:
            for turn in range(2):
                for index, step in enumerate(STEPS):
                    if step in steps:
                        x_copy(index, turn, c).start()

    depart(TRAVEL[:1])
    own(0)
    halo(0).start()
    halo(1).start()
    own_est.start()
    depart(TRAVEL[1:2])
    for c in range(1, AHEAD):
        own(c)
    depart(TRAVEL[2:])

    block, plane_row = position // ZB, position % ZB
    blank = jnp.zeros((VIEWS, 128 - TAPS), jnp.float32)
    columns = []
    for axis in range(2):
        taps = psf_ref[:, axis, :]
        taps = taps / jnp.sum(taps, axis=1, keepdims=True)
        columns.append(jnp.transpose(jnp.concatenate([taps, blank], axis=1)))
    tap = lax.broadcasted_iota(jnp.int32, (128, 256), 0)
    lane = lax.broadcasted_iota(jnp.int32, (128, 256), 1)
    total = jnp.zeros((VIEWS, 256), jnp.float32)
    for k in range(VIEWS):
        live = jnp.where(plane_row < lengths_ref[block, k], 1.0, 0.0)
        total = total + live
        dx, dy = offsets_ref[0, k], offsets_ref[1, k]
        places = ((0, lane - 16 - dx), (1, 224 - lane - dy), (1, lane - 160 - dy))
        for kind, (axis, place) in enumerate(places):
            column = jnp.broadcast_to(columns[axis][:, k : k + 1], (128, 256))
            line = jnp.sum(jnp.where(place == tap, column, 0.0), axis=0, keepdims=True)
            if kind == 2:
                line = line * live
            taps_ref[kind * VIEWS + k : kind * VIEWS + k + 1, :] = line
    taps_ref[3 * VIEWS : 4 * VIEWS, :] = total

    @pl.loop(0, VIEWS)
    def _(k):
        row = jnp.broadcast_to(taps_ref[pl.ds(k, 1), :], (TILE, 256))
        band = pltpu.roll(row, 0, 1, stride=1, stride_axis=0)
        rows_x[k] = band
        high, low = split(band)
        band_x[k, 0:TILE, :] = high
        band_x[k, TILE : 2 * TILE, :] = low
        for first, target in ((VIEWS, band_f), (2 * VIEWS, band_b)):
            row = jnp.broadcast_to(taps_ref[pl.ds(first + k, 1), :], (256, 256))
            band = pltpu.roll(row, 0, 1, stride=1, stride_axis=0)[:, :128]
            high, low = split(band)
            target[k, :, 0:128] = high
            target[k, :, 128:256] = low

    for g in range(GROUPS):
        first, second = ORDER[2 * g] * UNIT, ORDER[2 * g + 1] * UNIT
        picked = jnp.concatenate(
            [rows_x[:, first : first + UNIT, :], rows_x[:, second : second + UNIT, :]], axis=1)
        band = jnp.transpose(picked.reshape(256, 256))
        high, low = split(band)
        if g < GROUPS - 1:
            band_xt[g, 0:256, :] = high
            band_xt[g, 256:512, :] = low
        else:
            band_xt[g, 0:TILE, :] = high[REACH : REACH + TILE]
            band_xt[g, TILE : 2 * TILE, :] = low[REACH : REACH + TILE]

    def estimate():
        own_est.wait()
        halo(0).wait_recv()
        halo(1).wait_recv()
        est[SPAN:256, :] = jnp.zeros((256 - SPAN, COLS), jnp.float32)

        @pl.loop(0, 256 // 32)
        def _(i):
            rows = pl.ds(pl.multiple_of(i * 32, 32), 32)
            high, low = split(pltpu.roll(est[rows, :], 64, 1))
            est_hi[rows, 0:COLS] = high
            est_lo[rows, 0:COLS] = low
            est_hi[rows, COLS:PADDED] = high[:, 0:128]
            est_lo[rows, COLS:PADDED] = low[:, 0:128]

        count = jnp.broadcast_to(taps_ref[3 * VIEWS : 3 * VIEWS + 1, 0:1], (TILE, 1))
        est[REACH : REACH + TILE, :] = est[REACH : REACH + TILE, :] / count

    def forward(k):
        for first in range(0, PADDED, 256):
            width = min(256, PADDED - first)
            cols = pl.ds(first, width)
            wide = dot(band_x[k], est_hi[:, cols])
            value = wide[:TILE] + wide[TILE:] + dot(band_x[k, 0:TILE, :], est_lo[:, cols])
            high, low = split(value)
            for part in range(width // 128):
                b = first // 128 + part
                piece = slice(128 * part, 128 * part + 128)
                if b < 16:
                    win_hi[b, :, 0:128] = high[:, piece]
                    win_lo[b, :, 0:128] = low[:, piece]
                if b > 0:
                    win_hi[b - 1, :, 128:256] = high[:, piece]
                    win_lo[b - 1, :, 128:256] = low[:, piece]
        for b in range(0, 16, 4):
            wide = dot(win_hi[b : b + 4].reshape(512, 256), band_f[k])
            value = wide[:, :128] + wide[:, 128:]
            value = value + dot(win_lo[b : b + 4].reshape(512, 256), band_f[k, :, 0:128])
            for part in range(4):
                image[k, :, 128 * (b + part) : 128 * (b + part) + 128] = value[
                    128 * part : 128 * part + 128]

    def back_y(c, near):
        start = ORDER[c] * UNIT

        far = (0, 1, 3, 2)[near]

        @pl.loop(0, 2)
        def _(turn):
            k = 2 * ((y + far) % 4) + turn
            arrived(k, c)
            rows = slice(start, start + UNIT)
            ratio = arr[k, rows, :] / image[k, rows, :]
            high, low = split(pltpu.roll(ratio, 64, 1))
            for b in range(16):
                piece = slice(128 * b, 128 * b + 128)
                before = (b - 1) % 16
                bwin_hi[b, :, 0:128] = high[:, piece]
                bwin_lo[b, :, 0:128] = low[:, piece]
                bwin_hi[before, :, 128:256] = high[:, piece]
                bwin_lo[before, :, 128:256] = low[:, piece]
            wide = dot(bwin_hi[...].reshape(256, 256), band_b[k])
            value = wide[:, :128] + wide[:, 128:]
            value = value + dot(bwin_lo[...].reshape(256, 256), band_b[k, :, 0:128])
            high, low = split(value)
            into = slice((c % 2) * UNIT, (c % 2) * UNIT + UNIT)
            for b in range(16):
                spread_hi[k, into, 128 * b : 128 * b + 128] = high[16 * b : 16 * b + 16]
                spread_lo[k, into, 128 * b : 128 * b + 128] = low[16 * b : 16 * b + 16]

    def back_x(g, half):
        for start in range(half * COLS // 2, (half + 1) * COLS // 2, 256):
            cols = slice(start, start + 256)
            high = spread_hi[:, :, cols].reshape(256, 256)
            low = spread_lo[:, :, cols].reshape(256, 256)
            wide = dot(band_xt[g], high)
            value = wide[:256] + wide[256:] + dot(band_xt[g, 0:256, :], low)
            if g == 0:
                acc[:, cols] = value
            else:
                acc[:, cols] += value

    def last_x(half):
        g = GROUPS - 1
        for start in range(half * COLS // 2, (half + 1) * COLS // 2, 256):
            cols = slice(start, start + 256)
            high = spread_hi[:, :, cols].reshape(256, 256)
            low = spread_lo[:, :, cols].reshape(256, 256)
            wide = dot(band_xt[g, 0 : 2 * TILE, :], high)
            value = wide[:TILE] + wide[TILE:] + dot(band_xt[g, 0:TILE, :], low)
            value = value + acc[REACH : REACH + TILE, cols]
            value = value * est[REACH : REACH + TILE, cols]
            out_ref[0, :, cols] = value

    def edge(side):
        if side == 0:
            return pltpu.make_async_remote_copy(
                acc.at[pl.ds(REACH + TILE, REACH)], edges.at[0],
                cs_sem.at[0], c_sem.at[0], device_id=(up, position), device_id_type=MESH)
        return pltpu.make_async_remote_copy(
            acc.at[pl.ds(0, REACH)], edges.at[1],
            cs_sem.at[1], c_sem.at[1], device_id=(down, position), device_id_type=MESH)

    def sent(c):
        for turn in range(2):
            for index in range(3):
                x_copy(index, turn, c).wait_send()
            for step in range(4):
                _, _, _, y2, _ = y_route(step, turn, c)

                @pl.when(y2 != y)
                def _():
                    y_copy(step, turn, c).wait_send()

    for item in PLAN:
        if item[0] == "own":
            own(item[1])
        elif item[0] == "relay":
            relay(*item[1:])
        elif item[0] == "estimate":
            estimate()
        elif item[0] == "forward":
            forward(item[1])
        elif item[0] == "y":
            if item[1:] == (CHUNKS - 1, 0):
                halo(0).wait_send()
                halo(1).wait_send()
                for c in range(CHUNKS - 2):
                    sent(c)
            if item[1:] == (CHUNKS - 1, 3):
                edge(0).wait_recv()
                edge(1).wait_recv()
                acc[REACH : 2 * REACH, :] += edges[0]
                acc[TILE : REACH + TILE, :] += edges[1]
                edge(0).wait_send()
                edge(1).wait_send()
                sent(CHUNKS - 2)
            back_y(*item[1:])
        elif item[0] == "edge":
            edge(0).start()
            edge(1).start()
        elif item[1] < GROUPS - 1:
            back_x(*item[1:])
        else:
            last_x(item[2])

    sent(CHUNKS - 1)


def per_device(estimate, views, psf, offsets, lengths):
    operands = (estimate, views, psf, offsets.T, lengths.T)
    f32, bf16 = jnp.float32, jnp.bfloat16
    anywhere = pl.BlockSpec(memory_space=pl.ANY)
    vmem = pl.BlockSpec(memory_space=pltpu.VMEM)
    smem = pl.BlockSpec(memory_space=pltpu.SMEM)
    dma = pltpu.SemaphoreType.DMA
    return pl.pallas_call(
        kernel,
        out_shape=jax.ShapeDtypeStruct(estimate.shape, f32),
        in_specs=[anywhere, anywhere, vmem, smem, smem],
        out_specs=vmem,
        scratch_shapes=[
            pltpu.VMEM((2 * VIEWS, TILE, COLS), f32),
            pltpu.VMEM((VIEWS, TILE, COLS), f32),
            pltpu.VMEM((256, COLS), f32),
            pltpu.VMEM((256, PADDED), bf16),
            pltpu.VMEM((256, PADDED), bf16),
            pltpu.VMEM((16, TILE, 256), bf16),
            pltpu.VMEM((16, TILE, 256), bf16),
            pltpu.VMEM((16, UNIT, 256), bf16),
            pltpu.VMEM((16, UNIT, 256), bf16),
            pltpu.VMEM((VIEWS, 2 * UNIT, COLS), bf16),
            pltpu.VMEM((VIEWS, 2 * UNIT, COLS), bf16),
            pltpu.VMEM((256, COLS), f32),
            pltpu.VMEM((2, REACH, COLS), f32),
            pltpu.VMEM((VIEWS, 2 * TILE, 256), bf16),
            pltpu.VMEM((GROUPS, 512, 256), bf16),
            pltpu.VMEM((VIEWS, 256, 256), bf16),
            pltpu.VMEM((VIEWS, 256, 256), bf16),
            pltpu.VMEM((VIEWS, TILE, 256), f32),
            pltpu.VMEM((4 * VIEWS, 256), f32),
            dma((3, 2, CHUNKS)),
            dma((4, 2, CHUNKS)),
            dma((2 * VIEWS, CHUNKS)),
            dma((2,)),
            dma((2,)),
            dma((2,)),
            dma((2,)),
            dma,
        ],
        compiler_params=pltpu.CompilerParams(
            collective_id=0, has_side_effects=True, vmem_limit_bytes=50 * 2**20
        ),
        name="deconvolve",
    )(*(pltpu.with_memory_space_constraint(a, pltpu.HBM) for a in operands))


def solution(mesh):
    return jax.shard_map(
        per_device,
        mesh=mesh,
        in_specs=(P("view", "joined", None), P("view", None, "joined", None), P(), P(), P()),
        out_specs=P("view", "joined", None),
        check_vma=False,
    )
```
